32 devices in a mesh: band: 4 (over z), ga: 8 (over y, x, core).
Axes of the slice: x: 2, y: 2, z: 4, core: 2. Of those that a mesh axis runs over, the one named last changes fastest.
Arguments:
- coeffs: float32 [2, 4, 18432], P(None, 'band', 'ga'), may hold values from -8 to 8
- cell_map: int32 [18432], P('ga'), may hold values from 0 to 110591, as said below
- potential: float32 [96, 96, 96], P(None, 'ga'), may hold values from -2 to 1
- projectors: float32 [2, 64, 18432], P(None, None, 'ga'), may hold values from -6 to 6
- strengths: float32 [8, 8, 8], replicated, may hold values from -2 to 2
- proj_atom: int32 [64], replicated, may hold values from 0 to 7, as said below
- proj_chan: int32 [64], replicated, may hold values from 0 to 7, as said below
Outputs:
- new_bands: float32 [2, 4, 18432], P(None, 'band', 'ga')
- energy: float32 [4], P('band')
- residual_norm: float32 [4], P('band')
- correlation: float32 [2, 4, 4], P(None, 'band')
- subspace: float32 [2, 4, 4], P(None, 'band')
The draws below stay inside these ranges and needn't reach their ends.
Inputs may be any that keep to these rules, and one draw needn't show every extreme that they name: `cell_map`: in block d (entries d * 2304 to (d + 1) * 2304 - 1) the entries are distinct cells (i * 96 + y) * 96 + z of grid planes x = d + 8 * i. `proj_atom`: each pair of atom and channel belongs to exactly one projector. `proj_chan`: each pair of atom and channel belongs to exactly one projector.
All inputs are finite; a program needn't handle non-finite values.
Results may differ from the reference program's by a relative error of at most 0.0002.
Values sent between devices are 32-bit elements; how exact they have to be, the bound alone decides.
No kernel may reach another device: no remote copies, remote signals or barrier semaphores. Data moves between devices by JAX's collectives and lax.ppermute only.
A program may use at most 64 MiB of HBM per device.

```python
import jax
import jax.numpy as jnp
from jax import lax

NG = 96
PW_DEV = 2304
NATOM = 8
NCH = 8
NPROJ = 64
PW_BLOCKS = 8
NPW = 18432
NBANDS = 4


kin_unit = 0.02


def signed_freq_drawn(index_arr):
    return jnp.where(index_arr < NG // 2, index_arr, index_arr - NG)


def sphere_cells(key):
    block_count = NPW // PW_DEV
    planes = NG // block_count
    slab_cells = planes * NG * NG
    cell_ids = jnp.arange(slab_cells, dtype=jnp.int32)
    plane_num = cell_ids // (NG * NG)
    freq_y = signed_freq_drawn(cell_ids // NG % NG)
    freq_z = signed_freq_drawn(cell_ids % NG)

    def pick_cells(block_key, block_num):
        freq_x = signed_freq_drawn(block_num + block_count * plane_num)
        radius_sq = freq_x * freq_x + freq_y * freq_y + freq_z * freq_z
        jitter_key, order_key = jax.random.split(block_key)
        jitter_score = radius_sq * 8 + jax.random.randint(jitter_key, (slab_cells,), 0, 192, dtype=jnp.int32)
        chosen = jnp.argsort(jitter_score, stable=True)[:PW_DEV]
        shuffle = jax.random.permutation(order_key, PW_DEV)
        return chosen[shuffle].astype(jnp.int32)
    block_keys = jax.random.split(key, block_count)
    block_nums = jnp.arange(block_count, dtype=jnp.int32)
    return jax.vmap(pick_cells)(block_keys, block_nums).reshape(NPW)


def cell_energy(cells):
    block_count = NPW // PW_DEV
    owner = jnp.arange(NPW, dtype=jnp.int32) // PW_DEV
    freq_x = signed_freq_drawn(owner + block_count * (cells // (NG * NG)))
    freq_y = signed_freq_drawn(cells // NG % NG)
    freq_z = signed_freq_drawn(cells % NG)
    return kin_unit * (freq_x * freq_x + freq_y * freq_y + freq_z * freq_z).astype(jnp.float32)


def projector_values(key):
    cells = sphere_cells(jax.random.fold_in(key, 11))
    energy = cell_energy(cells)
    shape_key, scale_key = jax.random.split(jax.random.fold_in(key, 23))
    raw_values = jax.random.truncated_normal(shape_key, -6.0, 6.0, (2, NPROJ, NPW), jnp.float32)
    row_scale = jnp.exp(jax.random.uniform(scale_key, (NPROJ,), jnp.float32, -0.7, 0.7))
    shaped = raw_values * row_scale[None, :, None] / (1.0 + energy / 8.0)[None, None, :]
    return (jnp.clip(shaped, -6.0, 6.0), energy)


def draw_cell_map(key, part):
    return sphere_cells(jax.random.fold_in(key, 11))


def draw_projectors(key, part):
    return projector_values(key)[0]


def draw_coeffs(key, part):
    projectors, energy = projector_values(key)
    noise_key, mix_key, common_key, scale_key = jax.random.split(jax.random.fold_in(key, 37), 4)
    envelope = 1.0 / (1.0 + energy / 4.0)
    noise = jax.random.truncated_normal(noise_key, -6.0, 6.0, (2, NBANDS, NPW), jnp.float32)
    mixing = jax.random.truncated_normal(mix_key, -4.0, 4.0, (2, NBANDS, NPROJ), jnp.float32) * (0.5 / NPROJ ** 0.5)
    along_re = jnp.einsum('bp,pg->bg', mixing[0], projectors[0]) - jnp.einsum('bp,pg->bg', mixing[1], projectors[1])
    along_im = jnp.einsum('bp,pg->bg', mixing[0], projectors[1]) + jnp.einsum('bp,pg->bg', mixing[1], projectors[0])
    values = noise * envelope[None, None, :] + jnp.stack([along_re, along_im])
    return jnp.clip(values, -8.0, 8.0)


def projector_slots(key):
    ordering = jax.random.permutation(jax.random.fold_in(key, 51), NPROJ).astype(jnp.int32)
    return (ordering // NCH, ordering % NCH)


def draw_proj_atom(key, part):
    return projector_slots(key)[0]


def draw_proj_chan(key, part):
    return projector_slots(key)[1]


def shard_levels(key, extent, cuts, low, top_value):
    loudness = 1.0
    for axis_at, shards_of in cuts:
        heights = jax.random.uniform(jax.random.fold_in(jax.random.fold_in(key, 6), axis_at), (shards_of,), jnp.float32, low / len(cuts), top_value / len(cuts))
        loudness = loudness * jnp.repeat(jnp.exp(heights), extent[axis_at] // shards_of).reshape((-1,) + (1,) * (len(extent) - 1 - axis_at))
    return loudness


def setup_inputs(seed: int = 0) -> dict:
    arg_keys = jax.random.split(jax.random.key(seed), 8)
    coeffs = draw_coeffs(jax.random.fold_in(arg_keys[7], 71), 0)
    cell_map = draw_cell_map(jax.random.fold_in(arg_keys[7], 71), 0)
    potential = jnp.clip(-2.0 + 3.0 * jax.random.uniform(arg_keys[2], (NG, NG, NG), jnp.float32) ** shard_levels(arg_keys[2], (NG, NG, NG), ((1, 8),), -0.2, 0.2), -2.0, 1.0)
    projectors = draw_projectors(jax.random.fold_in(arg_keys[7], 71), 0)
    strengths = jnp.clip(jax.random.uniform(arg_keys[4], (NATOM, NCH, NCH), jnp.float32, -2.0, 2.0), -2.0, 2.0)
    proj_atom = draw_proj_atom(jax.random.fold_in(arg_keys[7], 71), 0)
    proj_chan = draw_proj_chan(jax.random.fold_in(arg_keys[7], 71), 0)
    return dict(coeffs=coeffs, cell_map=cell_map, potential=potential, projectors=projectors, strengths=strengths, proj_atom=proj_atom, proj_chan=proj_chan)


top_precision = lax.Precision.HIGHEST
kin_unit = 0.02
small_eps = 1e-6


def signed_freq(index_arr):
    return jnp.where(index_arr < NG // 2, index_arr, index_arr - NG)


def coupling_matrix(proj_atom, proj_chan, strengths):
    symmetric = 0.5 * (strengths + jnp.swapaxes(strengths, 1, 2))
    atom_hot = (proj_atom[:, None] == jnp.arange(NATOM, dtype=jnp.int32)[None, :]).astype(jnp.float32)
    chan_hot = (proj_chan[:, None] == jnp.arange(NCH, dtype=jnp.int32)[None, :]).astype(jnp.float32)
    rows_d = jnp.einsum("pa,pc,acd->pd", atom_hot, chan_hot, symmetric, precision=top_precision)
    same_atom = jnp.dot(atom_hot, atom_hot.T, precision=top_precision, preferred_element_type=jnp.float32)
    return same_atom * jnp.dot(rows_d, chan_hot.T, precision=top_precision, preferred_element_type=jnp.float32)


def band_dot(left_vec, right_vec, weight):
    return jnp.sum(left_vec * right_vec * weight, axis=(0, 2)) / NPW


def per_band(values):
    return values[None, :, None]


def precondition(residual, kinetic, kin_level):
    x_ratio = kinetic[None, :] / (1.5 * kin_level[:, None] + 1.0)
    numer_poly = 27.0 + x_ratio * (18.0 + x_ratio * (12.0 + 8.0 * x_ratio))
    square = x_ratio * x_ratio
    return residual * (numer_poly / (numer_poly + 16.0 * square * square))[None]


def pair_products(left_vec, right_vec):
    def contract(first_part, second_part):
        return jnp.einsum("bg,cg->bc", first_part, second_part, precision=top_precision)
    real_part = contract(left_vec[0], right_vec[0]) + contract(left_vec[1], right_vec[1])
    imag_part = contract(left_vec[0], right_vec[1]) - contract(left_vec[1], right_vec[0])
    return jnp.stack([real_part, imag_part])


def local_one(vector, flat_cells, potential):
    values = vector[0] + 1j * vector[1]
    grid_g = jnp.zeros((NG * NG * NG,), values.dtype).at[flat_cells].set(values)
    space = jnp.fft.ifftn(grid_g.reshape(NG, NG, NG)) * potential
    back = jnp.fft.fftn(space).reshape(NG * NG * NG)[flat_cells]
    return jnp.stack([jnp.real(back), jnp.imag(back)])


def reference(coeffs, cell_map, potential, projectors, strengths, proj_atom, proj_chan):
    owner = jnp.arange(NPW, dtype=jnp.int32) // PW_DEV
    x_index = owner + PW_BLOCKS * (cell_map // (NG * NG))
    y_index = (cell_map // NG) % NG
    z_index = cell_map % NG
    flat_cells = (x_index * NG + y_index) * NG + z_index
    freq_x = signed_freq(x_index)
    freq_y = signed_freq(y_index)
    freq_z = signed_freq(z_index)
    kinetic = kin_unit * (freq_x * freq_x + freq_y * freq_y + freq_z * freq_z).astype(jnp.float32)
    kin_weight = kinetic[None, None, :]
    coupling = coupling_matrix(proj_atom, proj_chan, strengths)

    def contract(first_part, second_part):
        return jnp.einsum("pg,bg->pb", first_part, second_part, precision=top_precision)

    def spread(weights, proj_table):
        return jnp.einsum("pb,pg->bg", weights, proj_table, precision=top_precision)

    def apply_h(vectors):
        local_term = lax.map(lambda vector: local_one(vector, flat_cells, potential), jnp.swapaxes(vectors, 0, 1))
        local_term = jnp.swapaxes(local_term, 0, 1)
        proj_re = (contract(projectors[0], vectors[0]) + contract(projectors[1], vectors[1])) / NPW
        proj_im = (contract(projectors[0], vectors[1]) - contract(projectors[1], vectors[0])) / NPW
        mixed_re = jnp.dot(coupling, proj_re, precision=top_precision, preferred_element_type=jnp.float32)
        mixed_im = jnp.dot(coupling, proj_im, precision=top_precision, preferred_element_type=jnp.float32)
        out_re = spread(mixed_re, projectors[0]) - spread(mixed_im, projectors[1])
        out_im = spread(mixed_re, projectors[1]) + spread(mixed_im, projectors[0])
        return kin_weight * vectors + local_term + jnp.stack([out_re, out_im])

    h_zero = apply_h(coeffs)
    eps_zero = band_dot(coeffs, h_zero, 1.0) / (band_dot(coeffs, coeffs, 1.0) + small_eps)
    r_zero = h_zero - per_band(eps_zero) * coeffs
    level_zero = band_dot(r_zero, r_zero, kin_weight) / (band_dot(r_zero, r_zero, 1.0) + small_eps)
    p_zero = precondition(r_zero, kinetic, level_zero)
    g_zero = apply_h(p_zero)
    q_zero = g_zero - per_band(eps_zero) * p_zero
    lam_zero = -band_dot(r_zero, q_zero, 1.0) / (band_dot(q_zero, q_zero, 1.0) + small_eps)
    psi_one = coeffs + per_band(lam_zero) * p_zero
    h_one = h_zero + per_band(lam_zero) * g_zero
    eps_one = band_dot(psi_one, h_one, 1.0) / (band_dot(psi_one, psi_one, 1.0) + small_eps)
    r_one = h_one - per_band(eps_one) * psi_one
    change = r_zero - r_one
    weight_one = band_dot(r_zero, change, 1.0) / (band_dot(change, change, 1.0) + small_eps)
    step_mid = weight_one * lam_zero
    psi_mid = coeffs + per_band(step_mid) * p_zero
    h_mid = h_zero + per_band(step_mid) * g_zero
    r_mid = r_zero - per_band(weight_one) * change
    eps_mid = band_dot(psi_mid, h_mid, 1.0) / (band_dot(psi_mid, psi_mid, 1.0) + small_eps)
    level_mid = band_dot(r_mid, r_mid, kin_weight) / (band_dot(r_mid, r_mid, 1.0) + small_eps)
    p_one = precondition(r_mid, kinetic, level_mid)
    g_one = apply_h(p_one)
    q_one = g_one - per_band(eps_mid) * p_one
    lam_one = -band_dot(r_mid, q_one, 1.0) / (band_dot(q_one, q_one, 1.0) + small_eps)
    new_bands = psi_mid + per_band(lam_one) * p_one
    new_ham = h_mid + per_band(lam_one) * g_one
    norm_new = band_dot(new_bands, new_bands, 1.0) + small_eps
    energy = band_dot(new_bands, new_ham, 1.0) / norm_new
    residual = new_ham - per_band(energy) * new_bands
    residual_norm = band_dot(residual, residual, 1.0) / norm_new
    correlation = pair_products(new_bands, new_bands) / NPW
    subspace = pair_products(new_bands, new_ham) / NPW
    return new_bands, energy, residual_norm, correlation, subspace
```

```python
import jax
import jax.numpy as jnp
import numpy as np
from jax import lax
from jax.experimental import pallas as pl
from jax.experimental.pallas import tpu as pltpu
from jax.sharding import PartitionSpec as P

kin_unit = 0.02
small_eps = 1e-06
F32 = jnp.float32
BF16 = jnp.bfloat16
HI = lax.Precision.HIGHEST
NN = (((1,), (0,)), ((), ()))
NT = (((1,), (1,)), ((), ()))


def round_up(value, unit):
    return -(-value // unit) * unit


def split_np(table):
    hi = table.astype(np.float32).astype(jnp.bfloat16)
    lo = (table - hi.astype(np.float64)).astype(np.float32).astype(jnp.bfloat16)
    return np.stack([hi, lo])


def split(vals):
    hi = vals.astype(BF16)
    return hi, (vals - hi.astype(F32)).astype(BF16)


def mm(left, right, dims=NN):
    return lax.dot_general(left, right, dims, preferred_element_type=F32)


def mm3(left, right):
    return mm(left[0], right[0]) + (mm(left[0], right[1]) + mm(left[1], right[0]))


def call(kernel, out_shapes, scratch=()):
    return pl.pallas_call(
        kernel,
        out_shape=[jax.ShapeDtypeStruct(s, d) for s, d in out_shapes],
        scratch_shapes=list(scratch),
        compiler_params=pltpu.CompilerParams(vmem_limit_bytes=56 * 1024 * 1024),
    )


def lane_sum(vals):
    return jnp.sum(jnp.sum(vals, axis=1, keepdims=True), axis=0, keepdims=True)


def gram_form(gram, left_map, right_map, kin):
    running = 0.0
    for i, a in left_map.items():
        for j, b in right_map.items():
            running = running + a * b * gram[kin, min(i, j), max(i, j)]
    return running


def combine(terms):
    merged = {}
    for scalar, coefs in terms:
        for i, a in coefs.items():
            merged[i] = merged.get(i, 0.0) + scalar * a
    return merged


def ratio(gram, a, b, c, d, kin=False):
    return gram_form(gram, a, b, kin) / (gram_form(gram, c, d, False) + small_eps)


def pairs_of(first, last):
    return [
        (kin, i, j) for kin in (False, True) for j in range(first, last) for i in range(j + 1)
    ]


def stage_zero(gram):
    psi, ham = {0: 1.0}, {1: 1.0}
    eps = ratio(gram, psi, ham, psi, psi)
    res = combine([(1.0, ham), (-eps, psi)])
    level = ratio(gram, res, res, res, res, True)
    return eps, res, level


def stage_mid(gram):
    eps, res, _ = stage_zero(gram)
    psi, ham = {0: 1.0}, {1: 1.0}
    q = {3: 1.0, 2: -eps}
    lam = -ratio(gram, res, q, q, q)
    psi1 = combine([(1.0, psi), (lam, {2: 1.0})])
    ham1 = combine([(1.0, ham), (lam, {3: 1.0})])
    eps1 = ratio(gram, psi1, ham1, psi1, psi1)
    res1 = combine([(1.0, ham1), (-eps1, psi1)])
    change = combine([(1.0, res), (-1.0, res1)])
    weight = ratio(gram, res, change, change, change)
    step = weight * lam
    psim = combine([(1.0, psi), (step, {2: 1.0})])
    hamm = combine([(1.0, ham), (step, {3: 1.0})])
    resm = combine([(1.0, res), (-weight, change)])
    epsm = ratio(gram, psim, hamm, psim, psim)
    level = ratio(gram, resm, resm, resm, resm, True)
    return epsm, psim, hamm, resm, level


def spread(coefs, basis):
    running = 0.0
    for i, a in coefs.items():
        if not isinstance(a, float):
            a = a[0:1, 0:1]
        running = running + a * basis[i]
    return running


def precondition(residual, kinetic, level):
    x = kinetic / (1.5 * level[0:1, 0:1] + 1.0)
    numer = 27.0 + x * (18.0 + x * (12.0 + 8.0 * x))
    square = x * x
    return residual * (numer / (numer + 16.0 * square * square))


def body(coeffs, cell_map, potential, projectors, strengths, proj_atom, proj_chan):
    ga = lax.axis_size("ga")
    nband = lax.axis_size("band")
    n = potential.shape[0]
    planes = n // ga
    npw = coeffs.shape[2]
    total = npw * ga
    nproj = projectors.shape[1]
    rp = round_up(2 * planes, 8)
    lp = round_up(planes * n, 128)
    nq = lp // 128
    zp = round_up(n, 128)
    rows = ga * rp
    psl = round_up(2 * nproj, 128)
    assert psl == 128

    k = np.arange(n)
    ang = 2.0 * np.pi / n * (np.outer(k, k) % n)
    cos, sin = np.cos(ang), np.sin(ang)
    ytab = np.zeros((2 * rows, n))
    for s in range(ga):
        for yl in range(planes):
            y = s * planes + yl
            r = s * rp + yl
            ytab[r], ytab[r + planes] = cos[y], sin[y]
            ytab[rows + r], ytab[rows + r + planes] = -sin[y], cos[y]
    xf = np.block([[cos, -sin], [sin, cos]])
    xb = np.block([[cos, sin], [-sin, cos]]) / n
    zf = np.zeros((2 * zp, 2 * zp))
    zb = np.zeros((2 * zp, 2 * zp))
    zf[:n, :n], zf[:n, zp:zp + n], zf[zp:zp + n, :n], zf[zp:zp + n, zp:zp + n] = cos, sin, -sin, cos
    zb[:n, :n], zb[:n, zp:zp + n], zb[zp:zp + n, :n], zb[zp:zp + n, zp:zp + n] = cos, -sin, sin, cos
    zb = zb / n
    ytab, xf, xb, zf, zb = [jnp.asarray(split_np(t)) for t in (ytab, xf, xb, zf, zb)]

    device = lax.axis_index("ga")
    plane_num = cell_map // (n * n)
    y_index = cell_map // n % n
    z_index = cell_map % n

    def freq(idx):
        return jnp.where(2 * idx < n, idx, idx - n)

    fx, fy, fz = freq(device + ga * plane_num), freq(y_index), freq(z_index)
    kinetic = (kin_unit * (fx * fx + fy * fy + fz * fz).astype(F32))[None, :]
    ycell = y_index[None, :]
    col = (plane_num * n + z_index)[None, :]
    proj = projectors.reshape(2 * nproj, npw)
    pot = jnp.pad(jnp.transpose(potential, (1, 0, 2)), ((0, 0), (0, 0), (0, zp - n)))
    pot = pot.reshape(planes * n, zp)

    natom, nch = strengths.shape[:2]
    sym = 0.5 * (strengths + jnp.swapaxes(strengths, 1, 2))
    ahot = (proj_atom[:, None] == jnp.arange(natom)[None, :]).astype(F32)
    chot = (proj_chan[:, None] == jnp.arange(nch)[None, :]).astype(F32)
    slot = (ahot[:, :, None] * chot[:, None, :]).reshape(nproj, natom * nch)
    big = (jnp.eye(natom, dtype=F32)[:, None, :, None] * sym[:, :, None, :]).reshape(
        natom * nch, natom * nch
    )
    coup = jnp.dot(jnp.dot(slot, big, precision=HI), slot.T, precision=HI) / total
    none = jnp.zeros_like(coup)
    mix = jnp.concatenate(
        [jnp.block([[coup, none], [none, coup]]), jnp.block([[none, coup], [-coup, none]])], axis=1
    )

    def one_hot(col_ref):
        lanes = lax.broadcasted_iota(jnp.int32, (lp, npw), 0)
        return jnp.where(lanes == col_ref[...], 1.0, 0.0).astype(BF16)

    def scatter_to(out_ref, vec, tab, col_ref, proj_ref):
        wave = vec[0:1] * tab[0:rows] + vec[1:2] * tab[rows:2 * rows]
        both = jnp.concatenate(split(wave), axis=0)
        grid = mm(both, one_hot(col_ref), NT)
        grid = (grid[:rows] + grid[rows:]).reshape(ga, rp, lp)
        for q in range(nq):
            out_ref[:, q * rp:(q + 1) * rp, :] = grid[:, :, 128 * q:128 * (q + 1)]
        eight = jnp.concatenate([vec, jnp.zeros((6, npw), F32)], axis=0)
        sums = lax.dot_general(eight, proj_ref[...], NT, precision=HI, preferred_element_type=F32)
        out_ref[:, nq * rp:nq * rp + 8, :] = jnp.broadcast_to(sums[None], (ga, 8, 128))

    send_shape = ((ga, nq * rp + 8, 128), F32)

    def first_kernel(vec_ref, y_ref, col_ref, proj_ref, ytab_ref, send_ref, tab_ref):
        kk = lax.broadcasted_iota(jnp.int32, (n, npw), 0)
        hot = jnp.where(kk == y_ref[...], 1.0, 0.0).astype(BF16)
        tab_ref[...] = mm(ytab_ref[0], hot) + mm(ytab_ref[1], hot)
        scatter_to(send_ref, vec_ref[...], tab_ref[...], col_ref, proj_ref)

    def mid_kernel(in_ref, pot_ref, xf_ref, xb_ref, zf_ref, zb_ref, out_ref, sum_ref, buf_ref):
        sum_ref[...] = jnp.sum(in_ref[:, nq * rp:nq * rp + 8, :], axis=0)
        grid = jnp.concatenate([in_ref[:, q * rp:(q + 1) * rp, :] for q in range(nq)], axis=-1)
        grid = grid.reshape(rows, lp)
        for i in range(planes):
            piece = grid[:, i * n:(i + 1) * n]
            if zp > n:
                piece = jnp.concatenate([piece, jnp.zeros((rows, zp - n), F32)], axis=1)
            buf_ref[i * rows:(i + 1) * rows, :] = piece
        half = []
        for c in range(2):
            half.append(
                jnp.concatenate(
                    [buf_ref[pl.ds(c * planes + j, n, stride=rp), :] for j in range(planes)], axis=1
                )
            )
        vals = jnp.concatenate(half, axis=0)
        vals = mm3((xf_ref[0], xf_ref[1]), split(vals))

        def to_rows(v):
            re = jnp.concatenate([v[:n, j * zp:(j + 1) * zp] for j in range(planes)], axis=0)
            im = jnp.concatenate([v[n:, j * zp:(j + 1) * zp] for j in range(planes)], axis=0)
            return jnp.concatenate([re, im], axis=1)

        def to_lanes(v):
            re = jnp.concatenate([v[j * n:(j + 1) * n, :zp] for j in range(planes)], axis=1)
            im = jnp.concatenate([v[j * n:(j + 1) * n, zp:] for j in range(planes)], axis=1)
            return jnp.concatenate([re, im], axis=0)

        vals = mm3(split(to_rows(vals)), (zf_ref[0], zf_ref[1]))
        weight = pot_ref[...]
        vals = vals * jnp.concatenate([weight, weight], axis=1)
        vals = mm3(split(vals), (zb_ref[0], zb_ref[1]))
        vals = mm3((xb_ref[0], xb_ref[1]), split(to_lanes(vals)))
        if rp > 2 * planes:
            buf_ref[...] = jnp.zeros(buf_ref.shape, F32)
        for c in range(2):
            for j in range(planes):
                buf_ref[pl.ds(c * planes + j, n, stride=rp), :] = vals[
                    c * n:(c + 1) * n, j * zp:(j + 1) * zp
                ]
        pieces = [buf_ref[i * rows:(i + 1) * rows, :][:, :n] for i in range(planes)]
        if lp > planes * n:
            pieces.append(jnp.zeros((rows, lp - planes * n), F32))
        grid = jnp.concatenate(pieces, axis=1).reshape(ga, rp, lp)
        for q in range(nq):
            out_ref[:, q * rp:(q + 1) * rp, :] = grid[:, :, 128 * q:128 * (q + 1)]

    mid_call = call(
        mid_kernel,
        [((ga, nq * rp, 128), F32), ((8, 128), F32)],
        [pltpu.VMEM((n * rp, zp), F32)],
    )

    def gather_from(back_ref, sum_ref, vec, tab_ref, col_ref, proj_ref, mix_ref, kin_ref):
        grid = jnp.concatenate([back_ref[:, q * rp:(q + 1) * rp, :] for q in range(nq)], axis=-1)
        both = jnp.concatenate(split(grid.reshape(rows, lp)), axis=0)
        got = mm(both, one_hot(col_ref))
        got = (got[:rows] + got[rows:]) * (1.0 / n)
        local_re = jnp.sum(got * tab_ref[0:rows], axis=0, keepdims=True)
        local_im = jnp.sum(got * tab_ref[rows:2 * rows], axis=0, keepdims=True)
        mixed = lax.dot_general(
            sum_ref[...], mix_ref[...], NN, precision=HI, preferred_element_type=F32
        )
        straight, turned = mixed[:, :128], mixed[:, 128:]
        coef = jnp.concatenate(
            [
                straight[0:1] - turned[1:2],
                straight[1:2] + turned[0:1],
                jnp.zeros((6, 128), F32),
            ],
            axis=0,
        )
        non = lax.dot_general(coef, proj_ref[...], NN, precision=HI, preferred_element_type=F32)
        return kin_ref[...] * vec + jnp.concatenate([local_re, local_im], axis=0) + non[0:2]

    def gram_rows(basis, pairs, kin):
        sums = []
        for use_kin, i, j in pairs:
            prod = basis[i] * basis[j]
            sums.append(lane_sum(prod * kin if use_kin else prod))
        sums += [jnp.zeros((1, 1), F32)] * (round_up(len(sums), 8) - len(sums))
        return jnp.broadcast_to(jnp.concatenate(sums, axis=0), (len(sums), 128))

    def read_gram(refs):
        gram = {}
        for ref, pairs in refs:
            for at, key in enumerate(pairs):
                gram[key] = ref[at:at + 1, :] * (1.0 / total)
        return gram

    pairs_a, pairs_b = pairs_of(0, 2), pairs_of(2, 4)
    rows_a, rows_b = round_up(len(pairs_a), 8), round_up(len(pairs_b), 8)
    vec_shape = ((2, npw), F32)

    def exchange(vals):
        return lax.all_to_all(vals, "ga", split_axis=0, concat_axis=0, tiled=True)

    def local_trip(send):
        out, sums = mid_call(exchange(send), pot, xf, xb, zf, zb)
        return exchange(out), sums

    vec = coeffs.reshape(2, npw)
    send, tab = call(first_kernel, [send_shape, ((2 * rows, npw), F32)])(
        vec, ycell, col, proj, ytab
    )
    back, sums = local_trip(send)

    def third_a(back_ref, sum_ref, c_ref, tab_ref, col_ref, proj_ref, mix_ref, kin_ref, h_ref, g_ref):
        c = c_ref[...]
        h = gather_from(back_ref, sum_ref, c, tab_ref, col_ref, proj_ref, mix_ref, kin_ref)
        h_ref[...] = h
        g_ref[...] = gram_rows([c, h], pairs_a, kin_ref[...])

    h0, gram_a = call(third_a, [vec_shape, ((rows_a, 128), F32)])(
        back, sums, vec, tab, col, proj, mix, kinetic
    )
    gram_a = lax.psum(gram_a, "ga")

    def first_b(ga_ref, c_ref, h_ref, tab_ref, col_ref, proj_ref, kin_ref, send_ref, p_ref):
        gram = read_gram([(ga_ref, pairs_a)])
        _, res, level = stage_zero(gram)
        p = precondition(spread(res, [c_ref[...], h_ref[...]]), kin_ref[...], level)
        p_ref[...] = p
        scatter_to(send_ref, p, tab_ref[...], col_ref, proj_ref)

    send, p0 = call(first_b, [send_shape, vec_shape])(gram_a, vec, h0, tab, col, proj, kinetic)
    back, sums = local_trip(send)

    def third_b(
        back_ref, sum_ref, c_ref, h_ref, p_ref, tab_ref, col_ref, proj_ref, mix_ref, kin_ref, g_out, gr_ref
    ):
        p = p_ref[...]
        g = gather_from(back_ref, sum_ref, p, tab_ref, col_ref, proj_ref, mix_ref, kin_ref)
        g_out[...] = g
        gr_ref[...] = gram_rows([c_ref[...], h_ref[...], p, g], pairs_b, kin_ref[...])

    g0, gram_b = call(third_b, [vec_shape, ((rows_b, 128), F32)])(
        back, sums, vec, h0, p0, tab, col, proj, mix, kinetic
    )
    gram_b = lax.psum(gram_b, "ga")

    def first_c(
        ga_ref, gb_ref, c_ref, h_ref, p_ref, g_ref, tab_ref, col_ref, proj_ref, kin_ref,
        send_ref, all_ref, eps_ref,
    ):
        gram = read_gram([(ga_ref, pairs_a), (gb_ref, pairs_b)])
        epsm, psim, hamm, resm, level = stage_mid(gram)
        basis = [c_ref[...], h_ref[...], p_ref[...], g_ref[...]]
        p = precondition(spread(resm, basis), kin_ref[...], level)
        all_ref[0:2] = spread(psim, basis)
        all_ref[2:4] = spread(hamm, basis)
        all_ref[4:6] = p
        all_ref[6:8] = spread(resm, basis)
        eps_ref[...] = jnp.broadcast_to(epsm, (8, 128))
        scatter_to(send_ref, p, tab_ref[...], col_ref, proj_ref)

    send, trio, eps_mid = call(first_c, [send_shape, ((8, npw), F32), ((8, 128), F32)])(
        gram_a, gram_b, vec, h0, p0, g0, tab, col, proj, kinetic
    )
    others = lax.all_gather(trio, "band", axis=0, tiled=True)
    back, sums = local_trip(send)

    def third_c(
        back_ref, sum_ref, trio_ref, others_ref, tab_ref, col_ref, proj_ref, mix_ref, kin_ref, out_ref
    ):
        p = trio_ref[4:6]
        g = gather_from(back_ref, sum_ref, p, tab_ref, col_ref, proj_ref, mix_ref, kin_ref)
        own = jnp.concatenate([trio_ref[0:6], g], axis=0)
        cross = lax.dot_general(own, others_ref[...], NT, precision=HI, preferred_element_type=F32)
        mine = lax.dot_general(own, own, NT, precision=HI, preferred_element_type=F32)
        out_ref[...] = jnp.concatenate([cross, mine], axis=1)

    width = 8 * nband + 8
    (prods,) = call(third_c, [((8, width), F32)])(
        back, sums, trio, others, tab, col, proj, mix, kinetic
    )
    band = lax.axis_index("band")
    slots = jnp.where(
        jnp.arange(nband)[:, None, None] == band, jnp.concatenate([prods, eps_mid[:, :1] / ga * total], axis=1)[None], 0.0
    )
    slots = lax.psum(slots, ("band", "ga")) / total

    mine = slots[:, :, 8 * nband:8 * nband + 8]
    dots = mine.reshape(nband, 4, 2, 4, 2)
    dots = dots[:, :, 0, :, 0] + dots[:, :, 1, :, 1]
    eps_all = slots[:, 0, width]
    gram = {(False, i, j): dots[:, i, j] for i in range(4) for j in range(i, 4)}
    psim, hamm, pvec, gvec = {0: 1.0}, {1: 1.0}, {2: 1.0}, {3: 1.0}
    paired = slots[:, :, :8 * nband].reshape(nband, 4, 2, nband, 4, 2)
    paired = paired[:, :, 0, :, 3, 0] + paired[:, :, 1, :, 3, 1]
    same = jnp.arange(nband)[:, None, None] == jnp.arange(nband)[None, None, :]
    rdots = jnp.sum(jnp.where(same, paired, 0.0), axis=2)
    q = combine([(1.0, gvec), (-eps_all, pvec)])
    lam = -(rdots[:, 3] - eps_all * rdots[:, 2]) / (gram_form(gram, q, q, False) + small_eps)
    new = combine([(1.0, psim), (lam, pvec)])
    ham = combine([(1.0, hamm), (lam, gvec)])
    norm = gram_form(gram, new, new, False) + small_eps
    energy = gram_form(gram, new, ham, False) / norm
    resid = combine([(1.0, ham), (-energy, new)])
    residual_norm = gram_form(gram, resid, resid, False) / norm

    def pick(values):
        return jnp.sum(jnp.where(jnp.arange(nband) == band, values, 0.0))

    lam_own = pick(lam)
    new_bands = trio[0:2] + lam_own * trio[4:6]
    cross = jnp.sum(
        jnp.where(jnp.arange(nband)[:, None, None] == band, slots[:, :, :8 * nband], 0.0), axis=0
    ).reshape(4, 2, nband, 4, 2)
    re = cross[:, 0, :, :, 0] + cross[:, 1, :, :, 1]
    im = cross[:, 0, :, :, 1] - cross[:, 1, :, :, 0]

    def rows_of(t):
        over = t[0, :, 0] + lam * t[0, :, 2] + lam_own * (t[2, :, 0] + lam * t[2, :, 2])
        sub = t[0, :, 1] + lam * t[1, :, 2] + lam_own * (t[2, :, 1] + lam * t[3, :, 2])
        return over, sub

    over_re, sub_re = rows_of(re)
    over_im, sub_im = rows_of(im)
    correlation = jnp.stack([over_re, over_im])[:, None, :]
    subspace = jnp.stack([sub_re, sub_im])[:, None, :]
    return (
        new_bands[:, None, :],
        pick(energy)[None],
        pick(residual_norm)[None],
        correlation,
        subspace,
    )


def solution(mesh):
    placed = (
        P(None, "band", "ga"),
        P("ga"),
        P(None, "ga", None),
        P(None, None, "ga"),
        P(),
        P(),
        P(),
    )
    return jax.shard_map(
        body,
        mesh=mesh,
        in_specs=placed,
        out_specs=(
            P(None, "band", "ga"),
            P("band"),
            P("band"),
            P(None, "band", None),
            P(None, "band", None),
        ),
        check_vma=False,
    )
```
